32 devices in a mesh: fsdp: 8 (over z, x), dp: 4 (over y, core).
Axes of the slice: x: 2, y: 2, z: 4, core: 2. Of those that a mesh axis runs over, the one named last changes fastest.
Arguments:
- streams: bfloat16 [2, 32, 152, 768], P(None, ('fsdp', 'dp')), may hold values from -6 to 6
- page_starts: int32 [2, 32, 4], P(None, ('fsdp', 'dp')), may hold values from 0 to 151, as said below
- attn_in: bfloat16 [2, 2, 3, 768, 768], P(None, None, None, 'fsdp'), may hold values from -0.21875 to 0.21875
- attn_out: bfloat16 [2, 2, 768, 768], P(None, None, 'fsdp'), may hold values from -1.25 to 1.25
- ffn_up: bfloat16 [2, 768, 3072], P(None, 'fsdp'), may hold values from -0.21875 to 0.21875
- ffn_down: bfloat16 [2, 3072, 768], P(None, 'fsdp'), may hold values from -0.109375 to 0.109375
- gate_weight: bfloat16 [2, 768, 768], P(None, 'fsdp'), may hold values from -0.15625 to 0.15625
- gate_bias: bfloat16 [768], P('fsdp'), may hold values from -4 to 4
- norm_gain: bfloat16 [2, 3, 768], P(None, None, 'fsdp'), may hold values from 0.099609375 to 1.8984375
- norm_bias: bfloat16 [2, 3, 768], P(None, None, 'fsdp'), may hold values from -2 to 2
- cotangent: bfloat16 [2, 32, 152, 768], P(None, ('fsdp', 'dp')), may hold values from -6 to 6
Outputs:
- mixed_streams: bfloat16 [2, 32, 152, 768], P(None, ('fsdp', 'dp'))
- streams_grad: float32 [2, 32, 152, 768], P(None, ('fsdp', 'dp'))
- attn_in_grad: float32 [2, 2, 3, 768, 768], P(None, None, None, 'fsdp')
- attn_out_grad: float32 [2, 2, 768, 768], P(None, None, 'fsdp')
- ffn_up_grad: float32 [2, 768, 3072], P(None, 'fsdp')
- ffn_down_grad: float32 [2, 3072, 768], P(None, 'fsdp')
- gate_weight_grad: float32 [2, 768, 768], P(None, 'fsdp')
- gate_bias_grad: float32 [768], P('fsdp')
- norm_gain_grad: float32 [2, 3, 768], P(None, None, 'fsdp')
- norm_bias_grad: float32 [2, 3, 768], P(None, None, 'fsdp')
The draws below stay inside these ranges and needn't reach their ends.
Inputs may be any that keep to these rules, and one draw needn't show every extreme that they name: page_starts[s, r, 0] is 0 and each row's 4 starts rise strictly; a page runs from its start to the next start or to 152; text page p and visual page p of a row belong together.
All inputs are finite; a program needn't handle non-finite values.
Results may differ from the reference program's by a relative error of at most 0.024.
Values may be sent and summed in bfloat16 or wider, within the bound.
No kernel may reach another device: no remote copies, remote signals or barrier semaphores. Data moves between devices by JAX's collectives and lax.ppermute only.
A program may use at most 384 MiB of HBM per device.

```python
import jax
import jax.numpy as jnp
from jax import lax

D = 768
HEADS = 12
HEAD_DIM = 64
FF = 3072
SEQ = 152
PAGES = 4
ROWS = 32


def draw_page_starts(key, part):
    row_keys = jax.random.split(key, 2 * ROWS)

    def one_row(row_key):
        page_cuts = jax.random.permutation(row_key, SEQ - 1)[:PAGES - 1].astype(jnp.int32) + 1
        return jnp.concatenate([jnp.zeros((1,), jnp.int32), jnp.sort(page_cuts)])
    return jax.vmap(one_row)(row_keys).reshape(2, ROWS, PAGES)


def block_scale(key, shape, shards, least, top_value):
    def one(dim, shards_of):
        heights = jax.random.uniform(jax.random.fold_in(jax.random.fold_in(key, 6), dim), (shards_of,), jnp.float32, least / len(shards), top_value / len(shards))
        return jnp.repeat(jnp.exp(heights), shape[dim] // shards_of).reshape((-1,) + (1,) * (len(shape) - dim - 1))

    gain = one(*shards[0])
    for cut in shards[1:]:
        gain = gain * one(*cut)
    return gain


def gaussian(stream_key, shape, deviation, most, cuts=(), kind=jnp.bfloat16):
    factor_of = block_scale(stream_key, shape, cuts, -0.22, 0.18) if cuts else 1.0
    values = jax.random.normal(stream_key, shape, jnp.float32) * deviation * factor_of
    return jnp.minimum(jnp.maximum(values, -most), most).astype(kind)


def setup_inputs(seed: int = 0) -> dict:
    streams_of = jax.random.split(jax.random.key(seed), 12)
    return {
        "streams": gaussian(streams_of[0], (2, ROWS, SEQ, D), 1.0, 6.0, ((1, 32),)),
        "page_starts": draw_page_starts(jax.random.fold_in(streams_of[11], 71), 0),
        "attn_in": gaussian(streams_of[2], (2, 2, 3, D, D), D ** -0.5, 0.21875, ((3, 8),)),
        "attn_out": gaussian(streams_of[3], (2, 2, D, D), (D // 32) ** -0.5, 1.25, ((2, 8),)),
        "ffn_up": gaussian(streams_of[4], (2, D, FF), D ** -0.5, 0.21875, ((1, 8),)),
        "ffn_down": gaussian(streams_of[5], (2, FF, D), FF ** -0.5, 0.109375, ((1, 8),)),
        "gate_weight": gaussian(streams_of[6], (2, D, D), (2 * D) ** -0.5, 0.15625, ((1, 8),)),
        "gate_bias": gaussian(streams_of[7], (D,), 1.0, 4.0, ((0, 8),)),
        "norm_gain": jnp.clip(1.0 + 0.18 * jax.random.normal(streams_of[8], (2, 3, D), jnp.float32), 0.099609375, 1.8984375).astype(jnp.bfloat16),
        "norm_bias": gaussian(streams_of[9], (2, 3, D), 0.3, 2.0, ((2, 8),)),
        "cotangent": gaussian(streams_of[10], (2, ROWS, SEQ, D), 1.0, 6.0, ((1, 32),)),
    }


@jax.custom_vjp
def low(v):
    return lax.optimization_barrier(v.astype(jnp.bfloat16)).astype(jnp.float32)

@jax.custom_vjp
def low_back(v):
    return v

def low_keep(v):
    return (low(v), None)

def low_pass(kept, grad):
    return (grad,)

def back_keep(v):
    return (v, None)

def back_low(kept, grad):
    return (low(grad),)
low.defvjp(low_keep, low_pass)
low_back.defvjp(back_keep, back_low)
highest = lax.Precision.HIGHEST

def layer_norm(values, scale_gain, shift_bias):
    center = values - lax.optimization_barrier(jnp.mean(values, axis=-1, keepdims=True))
    spread = lax.optimization_barrier(jnp.mean(center * center, axis=-1, keepdims=True))
    return center * lax.rsqrt(spread + 1e-05) * scale_gain[:, None, None, :] + shift_bias[:, None, None, :]

def page_number(starts):
    places = jnp.arange(SEQ, dtype=jnp.int32)
    return lax.optimization_barrier(jnp.sum((starts[:, :, None, :] <= places[None, None, :, None]).astype(jnp.int32), axis=-1))

def project(inputs, weight):
    return jnp.einsum('srld,sde->srle', inputs, weight, precision=highest)

def split_heads(values):
    return values.reshape(values.shape[:3] + (HEADS, HEAD_DIM))

def attention(query_in, key_in, weights_in, weight_out, page_mask):
    queries = split_heads(low(low_back(project(query_in, weights_in[:, 0]))))
    keyset = split_heads(low(low_back(project(key_in, weights_in[:, 1]))))
    values = split_heads(low(low_back(project(key_in, weights_in[:, 2]))))
    scores = low_back(jnp.einsum('srqhe,srkhe->srhqk', queries, keyset, precision=highest) * 0.125)
    scores = jnp.where(page_mask[:, :, None], scores, -1000000000.0)
    attn_probs = low(jax.nn.softmax(scores, axis=-1))
    mixed_heads = jnp.einsum('srhqk,srkhe->srqhe', attn_probs, values, precision=highest)
    mixed_heads = low(low_back(mixed_heads.reshape(query_in.shape)))
    return low_back(project(mixed_heads, weight_out))

def layer(inputs, starts, attn_in, attn_out, ffn_up, ffn_down, gate_weight, gate_bias, norm_gain, norm_bias):
    page_ids = page_number(starts)
    cross_mask = page_ids[:, :, :, None] == page_ids[::-1][:, :, None, :]
    self_mask = page_ids[:, :, :, None] == page_ids[:, :, None, :]
    cross_out = attention(inputs, inputs[::-1], attn_in[:, 0], attn_out[:, 0], cross_mask)
    first_out = low(layer_norm(inputs + cross_out, norm_gain[:, 0], norm_bias[:, 0]))
    self_out = attention(first_out, first_out, attn_in[:, 1], attn_out[:, 1], self_mask)
    second = low(layer_norm(first_out + self_out, norm_gain[:, 1], norm_bias[:, 1]))
    hidden = low(jax.nn.gelu(low_back(project(second, ffn_up)), approximate=False))
    ffn_out = low_back(project(hidden, ffn_down))
    third_out = low(layer_norm(second + ffn_out, norm_gain[:, 2], norm_bias[:, 2]))
    gate_pre = jnp.einsum('srld,sde->rle', third_out, gate_weight, precision=highest) + gate_bias
    gate_open = jax.nn.sigmoid(low_back(gate_pre))
    return jnp.stack([third_out[0] + gate_open * third_out[1], third_out[1] + (1.0 - gate_open) * third_out[0]])

def reference(streams, page_starts, attn_in, attn_out, ffn_up, ffn_down, gate_weight, gate_bias, norm_gain, norm_bias, cotangent):
    weight_set = tuple((item.astype(jnp.float32) for item in (attn_in, attn_out, ffn_up, ffn_down, gate_weight, gate_bias, norm_gain, norm_bias)))
    row_data = jnp.moveaxis(streams.astype(jnp.float32), 1, 0)[:, :, None]
    row_starts = jnp.moveaxis(page_starts, 1, 0)[:, :, None]

    def forward(row_inputs, *weight_args):

        def one_row(row_pair):
            return layer(row_pair[0], row_pair[1], *weight_args)
        return lax.map(jax.checkpoint(one_row), (row_inputs, row_starts))
    layer_out, pullback = jax.vjp(forward, row_data, *weight_set)
    cot_rows = jnp.moveaxis(cotangent.astype(jnp.float32), 1, 0)[:, :, None]
    grad_all = pullback(cot_rows)
    mixed_streams = jnp.moveaxis(layer_out[:, :, 0], 0, 1).astype(jnp.bfloat16)
    streams_grad = jnp.moveaxis(grad_all[0][:, :, 0], 0, 1)
    return (mixed_streams, streams_grad, grad_all[1], grad_all[2], grad_all[3], grad_all[4], grad_all[5], grad_all[6], grad_all[7], grad_all[8])
```

```python
import jax
import jax.numpy as jnp
from jax import lax
from jax.sharding import PartitionSpec as P

HEAD_DIM = 64
BF = jnp.bfloat16
F32 = jnp.float32


def dot(a, b):
    return jnp.einsum("rld,de->rle", a, b, preferred_element_type=F32)


def dot_t(a, b):
    return jnp.einsum("rle,de->rld", a, b, preferred_element_type=F32)


def outer(a, b):
    return jnp.einsum("rld,rle->de", a, b, preferred_element_type=F32).astype(BF)


def norm_stats(pre):
    center = pre - jnp.mean(pre, axis=-1, keepdims=True)
    scale = lax.rsqrt(jnp.mean(center * center, axis=-1, keepdims=True) + 1e-05)
    return center * scale, scale


def norm(pre, gain, shift):
    hat, scale = norm_stats(pre)
    return (hat * gain + shift).astype(BF)


def norm_back(pre, gain, grad):
    hat, scale = norm_stats(pre)
    scaled = grad * gain
    mean_one = jnp.mean(scaled, axis=-1, keepdims=True)
    mean_hat = jnp.mean(scaled * hat, axis=-1, keepdims=True)
    grad_pre = (scaled - mean_one - hat * mean_hat) * scale
    return grad_pre, jnp.sum(grad * hat, axis=(0, 1)), jnp.sum(grad, axis=(0, 1))


def split_heads(values):
    return values.reshape(values.shape[:2] + (values.shape[2] // HEAD_DIM, HEAD_DIM))


def attend(queries, keyset, values, mask):
    scores = 0.125 * jnp.einsum(
        "rqhe,rkhe->rhqk", split_heads(queries), split_heads(keyset), preferred_element_type=F32
    )
    probs = jax.nn.softmax(jnp.where(mask[:, None], scores, -1000000000.0), axis=-1)
    mixed = jnp.einsum(
        "rhqk,rkhe->rqhe", probs.astype(BF), split_heads(values), preferred_element_type=F32
    )
    return probs, mixed.reshape(queries.shape).astype(BF)


def attend_back(probs, queries, keyset, values, grad_mixed):
    shape = queries.shape
    grad_mixed = split_heads(grad_mixed)
    grad_probs = jnp.einsum(
        "rqhe,rkhe->rhqk", grad_mixed, split_heads(values), preferred_element_type=F32
    )
    grad_values = jnp.einsum(
        "rhqk,rqhe->rkhe", probs.astype(BF), grad_mixed, preferred_element_type=F32
    )
    grad_scores = probs * (grad_probs - jnp.sum(probs * grad_probs, axis=-1, keepdims=True))
    grad_scores = grad_scores.astype(BF)
    grad_queries = 0.125 * jnp.einsum(
        "rhqk,rkhe->rqhe", grad_scores, split_heads(keyset), preferred_element_type=F32
    )
    grad_keys = 0.125 * jnp.einsum(
        "rhqk,rqhe->rkhe", grad_scores, split_heads(queries), preferred_element_type=F32
    )
    return tuple(g.reshape(shape).astype(BF) for g in (grad_queries, grad_keys, grad_values))


def page_number(starts, length):
    places = jnp.arange(length, dtype=jnp.int32)
    return jnp.sum((starts[..., None, :] <= places[:, None]).astype(jnp.int32), axis=-1)


def body(
    streams,
    page_starts,
    attn_in,
    attn_out,
    ffn_up,
    ffn_down,
    gate_weight,
    gate_bias,
    norm_gain,
    norm_bias,
    cotangent,
):
    groups = lax.axis_size("fsdp")
    members = lax.axis_size("dp")
    place = lax.axis_index("dp")
    kind = place % 2
    half = place // 2
    length, width = streams.shape[2:]
    part = width // 2
    rows_of = attn_in.shape[3]
    hid_rows = ffn_down.shape[1]
    hid_half = hid_rows // 2

    def swap_core(value):
        return lax.ppermute(value, "dp", [(i, i ^ 1) for i in range(members)])

    def swap_half(value):
        return lax.ppermute(value, "dp", [(i, i ^ 2) for i in range(members)])

    def in_order(flag, mine, other, axis):
        return jnp.where(
            flag == 0,
            jnp.concatenate([mine, other], axis),
            jnp.concatenate([other, mine], axis),
        )

    def pick(value, index, size, axis):
        return lax.dynamic_slice_in_dim(value, index * size, size, axis)

    def take(value, index, axis=0):
        return lax.dynamic_index_in_dim(value, index, axis, keepdims=False)

    def gather(value, axis):
        return lax.all_gather(value, "fsdp", axis=axis, tiled=True)

    def scatter(value, axis):
        return lax.psum_scatter(value, "fsdp", scatter_dimension=axis, tiled=True)

    def both_halves(value, axis):
        return in_order(half, value, swap_half(value), axis)

    pair = in_order(kind, streams, swap_core(streams), 1)
    rows = both_halves(pair, 1)
    cots = in_order(kind, cotangent, swap_core(cotangent), 1).astype(F32)
    starts = lax.all_gather(page_starts, "dp", axis=1, tiled=True)

    my_in = pick(take(attn_in, kind), half, part, 3)
    my_out = pick(take(attn_out, kind), half, part, 2)
    my_up = take(ffn_up, kind).reshape(rows_of, groups, 2, hid_half)
    my_up = take(my_up, half, 2).reshape(rows_of, groups * hid_half)
    my_down = pick(take(ffn_down, kind), half, hid_half, 0)
    my_gate = pick(take(gate_weight, kind), half, part, 1)
    small = jnp.concatenate(
        [take(norm_gain, kind), take(norm_bias, kind), gate_bias[None]], axis=0
    )
    small = gather(small, 1).astype(F32)
    cross_in = gather(my_in[0], 1)
    cross_out = both_halves(gather(my_out[0], 0), 1)
    self_in = gather(my_in[1], 1)
    self_out = both_halves(gather(my_out[1], 0), 1)
    up = gather(my_up, 0)
    down = gather(my_down, 0)
    gate = both_halves(gather(my_gate, 0), 1)
    gains, shifts, bias = small[:3], small[3:6], small[6]

    pages = page_number(starts, length)
    my_pages = take(pages, kind)
    other_pages = take(pages, 1 - kind)
    cross_mask = my_pages[:, :, None] == other_pages[:, None, :]
    self_mask = my_pages[:, :, None] == my_pages[:, None, :]

    def heads_to_rows(mixed):
        sent = swap_half(pick(mixed, 1 - half, 2, 0))
        return in_order(half, pick(mixed, half, 2, 0), sent, 2)

    def rows_to_heads(grad):
        sent = swap_half(pick(grad, 1 - half, part, 2))
        return in_order(half, pick(grad, half, part, 2), sent, 0)

    def sum_rows(partial):
        sent = swap_half(pick(partial, 1 - half, 2, 0).astype(BF))
        return pick(partial, half, 2, 0) + sent.astype(F32)

    def sum_columns(term):
        sent = swap_half(pick(term, 1 - half, part, 1))
        return (pick(term, half, part, 1).astype(F32) + sent.astype(F32)).astype(BF)

    asked = take(rows, kind)
    shown = take(rows, 1 - kind)
    own = pick(asked, half, 2, 0).astype(F32)

    cross_q = dot(asked, cross_in[0]).astype(BF)
    cross_k = dot(shown, cross_in[1]).astype(BF)
    cross_v = dot(shown, cross_in[2]).astype(BF)
    cross_p, mixed = attend(cross_q, cross_k, cross_v, cross_mask)
    cross_o = heads_to_rows(mixed)
    first_pre = own + dot(cross_o, cross_out)
    first = norm(first_pre, gains[0], shifts[0])
    first_all = both_halves(first, 0)

    self_q = dot(first_all, self_in[0]).astype(BF)
    self_k = dot(first_all, self_in[1]).astype(BF)
    self_v = dot(first_all, self_in[2]).astype(BF)
    self_p, mixed = attend(self_q, self_k, self_v, self_mask)
    self_o = heads_to_rows(mixed)
    second_pre = first.astype(F32) + dot(self_o, self_out)
    second = norm(second_pre, gains[1], shifts[1])
    second_all = both_halves(second, 0)

    hidden_pre = dot(second_all, up)
    hidden = jax.nn.gelu(hidden_pre, approximate=False).astype(BF)
    third_pre = second.astype(F32) + sum_rows(dot(hidden, down))
    third = norm(third_pre, gains[2], shifts[2])

    gate_part = dot(third, gate)
    third_other = swap_core(third)
    gate_open = jax.nn.sigmoid(gate_part + swap_core(gate_part) + bias)
    third_mine = third.astype(F32)
    third_other = third_other.astype(F32)
    text = jnp.where(kind == 0, third_mine, third_other)
    visual = jnp.where(kind == 0, third_other, third_mine)
    mixed_streams = jnp.stack(
        [text + gate_open * visual, visual + (1.0 - gate_open) * text]
    ).astype(BF)
    mixed_streams = pick(mixed_streams, kind, 1, 1)

    grad_third = jnp.where(
        kind == 0, cots[0] + (1.0 - gate_open) * cots[1], cots[1] + gate_open * cots[0]
    )
    grad_gate = (
        (cots[0] * visual - cots[1] * text) * gate_open * (1.0 - gate_open)
    ).astype(BF)
    bias_term = jnp.sum(grad_gate.astype(F32), axis=(0, 1))
    gate_term = scatter(sum_columns(outer(third, grad_gate)), 0)
    grad_third = grad_third + dot_t(grad_gate, gate)
    grad_third_pre, gain_three, shift_three = norm_back(third_pre, gains[2], grad_third)

    grad_ffn = both_halves(grad_third_pre.astype(BF), 0)
    down_term = scatter(outer(hidden, grad_ffn), 0)
    grad_hidden = dot_t(grad_ffn, down)
    grad_hidden_pre = jax.vjp(
        lambda value: jax.nn.gelu(value, approximate=False), hidden_pre
    )[1](grad_hidden)[0].astype(BF)
    up_term = scatter(outer(second_all, grad_hidden_pre), 0)
    grad_second = grad_third_pre + sum_rows(dot_t(grad_hidden_pre, up))
    grad_second_pre, gain_two, shift_two = norm_back(second_pre, gains[1], grad_second)

    grad_low = grad_second_pre.astype(BF)
    self_out_term = scatter(sum_columns(outer(self_o, grad_low)), 0)
    grad_mixed = rows_to_heads(dot_t(grad_low, self_out).astype(BF))
    grads = attend_back(self_p, self_q, self_k, self_v, grad_mixed)
    self_in_term = scatter(jnp.stack([outer(first_all, g) for g in grads]), 1)
    grad_first = grad_second_pre + sum_rows(
        dot_t(grads[0], self_in[0]) + dot_t(grads[1], self_in[1]) + dot_t(grads[2], self_in[2])
    )
    grad_first_pre, gain_one, shift_one = norm_back(first_pre, gains[0], grad_first)

    grad_low = grad_first_pre.astype(BF)
    cross_out_term = scatter(sum_columns(outer(cross_o, grad_low)), 0)
    grad_mixed = rows_to_heads(dot_t(grad_low, cross_out).astype(BF))
    grads = attend_back(cross_p, cross_q, cross_k, cross_v, grad_mixed)
    cross_in_term = scatter(
        jnp.stack(
            [outer(asked, grads[0]), outer(shown, grads[1]), outer(shown, grads[2])]
        ),
        1,
    )
    grad_shown = dot_t(grads[1], cross_in[1]) + dot_t(grads[2], cross_in[2])
    grad_asked = dot_t(grads[0], cross_in[0]) + swap_core(grad_shown)
    grad_rows = grad_first_pre + sum_rows(grad_asked)
    streams_grad = in_order(
        kind,
        pick(grad_rows, kind, 1, 0)[None],
        swap_core(pick(grad_rows, 1 - kind, 1, 0))[None],
        0,
    )

    terms = jnp.stack(
        [gain_one, gain_two, gain_three, shift_one, shift_two, shift_three, bias_term]
    )
    terms = scatter(terms, 1)
    terms = terms + swap_half(terms)

    def everywhere(value, axis):
        wide = both_halves(value, axis)
        return in_order(kind, wide[None], swap_core(wide)[None], 0).astype(F32)

    attn_in_grad = everywhere(jnp.stack([cross_in_term, self_in_term]), 3)
    attn_out_grad = everywhere(jnp.stack([cross_out_term, self_out_term]), 2)
    up_grad = everywhere(up_term.reshape(rows_of, groups, 1, hid_half), 2)
    up_grad = up_grad.reshape(ffn_up.shape)
    down_grad = everywhere(down_term, 0)
    gate_grad = everywhere(gate_term, 1)
    norm_terms = in_order(kind, terms[None, :6], swap_core(terms[:6])[None], 0)
    return (
        mixed_streams,
        streams_grad,
        attn_in_grad,
        attn_out_grad,
        up_grad,
        down_grad,
        gate_grad,
        terms[6],
        norm_terms[:, :3],
        norm_terms[:, 3:],
    )


def solution(mesh):
    rows = P(None, ("fsdp", "dp"), None, None)
    weights = (
        P(None, None, None, "fsdp", None),
        P(None, None, "fsdp", None),
        P(None, "fsdp", None),
        P(None, "fsdp", None),
        P(None, "fsdp", None),
        P("fsdp"),
        P(None, None, "fsdp"),
        P(None, None, "fsdp"),
    )
    return jax.shard_map(
        body,
        mesh=mesh,
        in_specs=(rows, P(None, ("fsdp", "dp"), None)) + weights + (rows,),
        out_specs=(rows, rows) + weights,
        check_vma=False,
    )
```

```python
import jax
import jax.numpy as jnp
from jax import lax
from jax.sharding import PartitionSpec as P

HEAD_DIM = 64
BF = jnp.bfloat16
F32 = jnp.float32


def dot(a, b):
    return jnp.einsum("rld,de->rle", a, b, preferred_element_type=F32)


def dot_t(a, b):
    return jnp.einsum("rle,de->rld", a, b, preferred_element_type=F32)


def outer(a, b):
    return jnp.einsum("rld,rle->de", a, b, preferred_element_type=F32).astype(BF)


def norm_stats(pre):
    center = pre - jnp.mean(pre, axis=-1, keepdims=True)
    scale = lax.rsqrt(jnp.mean(center * center, axis=-1, keepdims=True) + 1e-05)
    return center * scale, scale


def norm(pre, gain, shift):
    hat, scale = norm_stats(pre)
    return (hat * gain + shift).astype(BF)


def norm_back(pre, gain, grad):
    hat, scale = norm_stats(pre)
    scaled = grad * gain
    mean_one = jnp.mean(scaled, axis=-1, keepdims=True)
    mean_hat = jnp.mean(scaled * hat, axis=-1, keepdims=True)
    grad_pre = (scaled - mean_one - hat * mean_hat) * scale
    return grad_pre, jnp.sum(grad * hat, axis=(0, 1)), jnp.sum(grad, axis=(0, 1))


def split_heads(values):
    return values.reshape(values.shape[:2] + (values.shape[2] // HEAD_DIM, HEAD_DIM))


def attend(queries, keyset, values, mask):
    scores = 0.125 * jnp.einsum(
        "rqhe,rkhe->rhqk", split_heads(queries), split_heads(keyset), preferred_element_type=F32
    )
    probs = jax.nn.softmax(jnp.where(mask[:, None], scores, -1000000000.0), axis=-1)
    mixed = jnp.einsum(
        "rhqk,rkhe->rqhe", probs.astype(BF), split_heads(values), preferred_element_type=F32
    )
    return probs, mixed.reshape(queries.shape).astype(BF)


def attend_back(probs, queries, keyset, values, grad_mixed):
    shape = queries.shape
    grad_mixed = split_heads(grad_mixed)
    grad_probs = jnp.einsum(
        "rqhe,rkhe->rhqk", grad_mixed, split_heads(values), preferred_element_type=F32
    )
    grad_values = jnp.einsum(
        "rhqk,rqhe->rkhe", probs.astype(BF), grad_mixed, preferred_element_type=F32
    )
    grad_scores = probs * (grad_probs - jnp.sum(probs * grad_probs, axis=-1, keepdims=True))
    grad_scores = grad_scores.astype(BF)
    grad_queries = 0.125 * jnp.einsum(
        "rhqk,rkhe->rqhe", grad_scores, split_heads(keyset), preferred_element_type=F32
    )
    grad_keys = 0.125 * jnp.einsum(
        "rhqk,rqhe->rkhe", grad_scores, split_heads(queries), preferred_element_type=F32
    )
    return tuple(g.reshape(shape).astype(BF) for g in (grad_queries, grad_keys, grad_values))


def page_number(starts, length):
    places = jnp.arange(length, dtype=jnp.int32)
    return jnp.sum((starts[..., None, :] <= places[:, None]).astype(jnp.int32), axis=-1)


def lines_of(mesh):
    spots = [getattr(d, "coords", None) for d in mesh.devices[:, 0]]
    if spots[0] is None:
        return [len(spots)]
    spots = [tuple(s) for s in spots]
    sizes = []
    while len(spots) > 1:
        size = 2
        step = [b - a for a, b in zip(spots[0], spots[1])]
        while size < len(spots) and [b - a for a, b in zip(spots[size - 1], spots[size])] == step:
            size += 1
        sizes.append(size)
        spots = spots[::size]
    return sizes[::-1]


class Lines:
    def __init__(self, sizes):
        self.lines = []
        stride = 1
        for size in reversed(sizes):
            self.lines.append((size, stride))
            stride *= size
        self.lines.reverse()
        self.count = stride

    def move(self, value, pairs, size, stride):
        whole = []
        for base in range(self.count):
            if (base // stride) % size == 0:
                whole += [(base + a * stride, base + b * stride) for a, b in pairs]
        return lax.ppermute(value, "fsdp", whole)

    def pairs(self, size, span, swaps):
        return [(base + a, base + b) for base in range(0, size, span) for a, b in swaps]

    def spot(self, size, stride):
        return (lax.axis_index("fsdp") // stride) % size

    def gather_line(self, value, size, stride):
        spot = self.spot(size, stride)
        span = 2
        while span <= size:
            mid = span // 2
            got = self.move(
                value, self.pairs(size, span, [(mid - 1, mid), (mid, mid - 1)]), size, stride
            )
            other = got
            for step in range(1, mid):
                got = self.move(
                    got,
                    self.pairs(
                        size, span, [(mid - step, mid - step - 1), (mid + step - 1, mid + step)]
                    ),
                    size,
                    stride,
                )
                place = spot % span
                here = (place == mid - step - 1) | (place == mid + step)
                other = jnp.where(here, got, other)
            low = (spot % span) < mid
            value = jnp.where(
                low, jnp.concatenate([value, other], 0), jnp.concatenate([other, value], 0)
            )
            span *= 2
        return value

    def scatter_line(self, value, size, stride):
        spot = self.spot(size, stride)
        span = size
        while span >= 2:
            mid = span // 2
            low = (spot % span) < mid
            mine = jnp.where(low, value[:mid], value[mid:])
            away = jnp.where(low, value[mid:], value[:mid])
            for step in range(mid - 1, 0, -1):
                got = self.move(
                    away,
                    self.pairs(
                        size, span, [(mid - step - 1, mid - step), (mid + step, mid + step - 1)]
                    ),
                    size,
                    stride,
                )
                away = add(away, got)
            got = self.move(
                away, self.pairs(size, span, [(mid - 1, mid), (mid, mid - 1)]), size, stride
            )
            value = add(mine, got)
            span = mid
        return value

    def gather(self, value):
        value = value[None]
        for size, stride in self.lines:
            shape = value.shape
            value = self.gather_line(value[None], size, stride)
            value = jnp.moveaxis(value, 0, 1).reshape((-1,) + shape[1:])
        return value

    def scatter(self, value):
        for size, stride in reversed(self.lines):
            value = value.reshape((-1, size) + value.shape[1:])
            value = self.scatter_line(jnp.moveaxis(value, 1, 0), size, stride)[0]
        return value[0]


def add(a, b):
    return (a.astype(F32) + b.astype(F32)).astype(BF)


def body(
    lines,
    streams,
    page_starts,
    attn_in,
    attn_out,
    ffn_up,
    ffn_down,
    gate_weight,
    gate_bias,
    norm_gain,
    norm_bias,
    cotangent,
):
    groups = lax.axis_size("fsdp")
    members = lax.axis_size("dp")
    place = lax.axis_index("dp")
    half = place % 2
    kind = place // 2
    length, width = streams.shape[2:]
    part = width // 2
    rows_of = attn_in.shape[3]
    hid_rows = ffn_down.shape[1]
    hid_half = hid_rows // 2

    def swap_core(value):
        return lax.ppermute(value, "dp", [(i, i ^ 1) for i in range(members)])

    def swap_kind(value):
        return lax.ppermute(value, "dp", [(i, i ^ 2) for i in range(members)])

    def in_order(flag, mine, other, axis):
        return jnp.where(
            flag == 0,
            jnp.concatenate([mine, other], axis),
            jnp.concatenate([other, mine], axis),
        )

    def pick(value, index, size, axis):
        return lax.dynamic_slice_in_dim(value, index * size, size, axis)

    def take(value, index, axis=0):
        return lax.dynamic_index_in_dim(value, index, axis, keepdims=False)

    def both_halves(value, axis):
        return in_order(half, value, swap_core(value), axis)

    def with_partner(value):
        return jnp.concatenate([value, swap_core(value)], 0)

    def by_kind(value):
        return jnp.stack([take(value, kind), take(value, 1 - kind)])

    home = by_kind(streams)[:, 0]
    cots = by_kind(cotangent)[:, 0].astype(F32)
    starts = jnp.broadcast_to(
        page_starts.reshape(2, 1, 1, -1).astype(BF), (2, 1, 8, page_starts.shape[2])
    )
    starts = jnp.pad(starts, ((0, 0), (0, 0), (0, 0), (0, width - page_starts.shape[2])))
    home = jnp.concatenate([home, by_kind(starts)[:, 0]], 1)
    away = swap_kind(home)[::-1]
    two = jnp.stack([home, away], 1)
    four = jnp.concatenate([two, swap_core(two)], 1)
    asked, shown = four[0, :, :length], four[1, :, :length]
    starts = four[:, :, length, : page_starts.shape[2]].astype(jnp.int32)
    pages = page_number(starts, length)
    cross_mask = pages[0, :, :, None] == pages[1, :, None, :]
    self_mask = pages[0, :, :, None] == pages[0, :, None, :]

    my_in = pick(take(attn_in, kind), half, part, 3)
    my_out = pick(take(attn_out, kind), half, part, 2)
    my_up = take(ffn_up, kind).reshape(rows_of, groups, 2, hid_half)
    my_up = take(my_up, half, 2).reshape(rows_of, -1, part)
    my_up = jnp.moveaxis(my_up, 1, 0)
    parts_up = my_up.shape[0]
    my_down = pick(take(ffn_down, kind), half, hid_half, 0)
    my_gate = pick(take(gate_weight, kind), half, part, 1)
    small = jnp.concatenate([take(norm_gain, kind), take(norm_bias, kind), gate_bias[None]], 0)
    small_rows = -(-7 * rows_of // part)
    small = jnp.pad(small.reshape(-1), (0, small_rows * part - 7 * rows_of)).reshape(-1, part)

    def blocks(gathered, index):
        return gathered[:, index * rows_of : (index + 1) * rows_of].reshape(-1, part)

    got = lines.gather(jnp.concatenate([my_in[0].reshape(-1, part), small], 0))
    cross_in = [blocks(got, i) for i in range(3)]
    small = got[:, 3 * rows_of :].reshape(groups, -1)[:, : 7 * rows_of]
    small = jnp.moveaxis(small.reshape(groups, 7, rows_of), 0, 1).reshape(7, width).astype(F32)
    gains, shifts, bias = small[:3], small[3:6], small[6]
    got = lines.gather(jnp.concatenate([my_out[0], my_in[1].reshape(-1, part)], 0))
    cross_out = both_halves(blocks(got, 0), 1)
    self_in = [blocks(got, 1 + i) for i in range(3)]
    got = lines.gather(jnp.concatenate([my_out[1], my_up.reshape(-1, part)], 0))
    self_out = both_halves(blocks(got, 0), 1)
    up = [blocks(got, 1 + i) for i in range(parts_up)]
    down_rows = hid_half
    got = lines.gather(jnp.concatenate([my_down[:, :part], my_down[:, part:], my_gate], 0))
    down = [
        got[:, :down_rows].reshape(-1, part),
        got[:, down_rows : 2 * down_rows].reshape(-1, part),
    ]
    gate = both_halves(got[:, 2 * down_rows :].reshape(-1, part), 1)
    gate_other = swap_kind(gate)
    up = jnp.concatenate(up, 1)
    down = jnp.concatenate(down, 1)

    def heads_to_rows(mixed):
        return in_order(half, mixed[:2], swap_core(mixed[2:]), 2)

    def rows_to_heads(grad):
        sent = swap_core(pick(grad, 1 - half, part, 2))
        return jnp.concatenate([pick(grad, half, part, 2), sent], 0)

    def sum_rows(partial):
        return partial[:2] + swap_core(partial[2:].astype(BF)).astype(F32)

    def sum_columns(term):
        return add(pick(term, half, part, 1), swap_core(pick(term, 1 - half, part, 1)))

    own = asked[:2].astype(F32)
    cross_q = dot(asked, cross_in[0]).astype(BF)
    cross_k = dot(shown, cross_in[1]).astype(BF)
    cross_v = dot(shown, cross_in[2]).astype(BF)
    cross_p, mixed = attend(cross_q, cross_k, cross_v, cross_mask)
    cross_o = heads_to_rows(mixed)
    first_pre = own + dot(cross_o, cross_out)
    first = norm(first_pre, gains[0], shifts[0])
    first_all = with_partner(first)

    self_q = dot(first_all, self_in[0]).astype(BF)
    self_k = dot(first_all, self_in[1]).astype(BF)
    self_v = dot(first_all, self_in[2]).astype(BF)
    self_p, mixed = attend(self_q, self_k, self_v, self_mask)
    self_o = heads_to_rows(mixed)
    second_pre = first.astype(F32) + dot(self_o, self_out)
    second = norm(second_pre, gains[1], shifts[1])
    second_all = with_partner(second)

    hidden_pre = dot(second_all, up)
    hidden = jax.nn.gelu(hidden_pre, approximate=False).astype(BF)
    third_pre = second.astype(F32) + sum_rows(dot(hidden, down))
    third = norm(third_pre, gains[2], shifts[2])

    sign = jnp.where(kind == 0, 1.0, -1.0)
    third_home = third[:1]
    third_other = swap_kind(third[1:])
    gate_open = jax.nn.sigmoid(
        sign * (dot(third_home, gate) + dot(third_other, gate_other) + bias)
    )
    text, visual = third_home.astype(F32), third_other.astype(F32)
    mixed_mine = (text + gate_open * visual).astype(BF)
    mixed_other = (visual + (1.0 - gate_open) * text).astype(BF)
    mixed_streams = in_order(kind, mixed_mine[None], mixed_other[None], 0)
    cot_mine, cot_other = cots[:1], cots[1:]
    grad_gate = (
        sign * (cot_mine * visual - cot_other * text) * gate_open * (1.0 - gate_open)
    ).astype(BF)
    bias_term = jnp.sum(grad_gate.astype(F32), axis=(0, 1))
    grad_mine = cot_mine + (1.0 - gate_open) * cot_other + dot_t(grad_gate, gate)
    grad_other = cot_other + gate_open * cot_mine + dot_t(grad_gate, gate_other)
    grad_third = jnp.concatenate(
        [grad_mine, swap_kind(grad_other.astype(BF)).astype(F32)], 0
    )
    grad_gates = jnp.concatenate([grad_gate, swap_kind(grad_gate)], 0)
    gate_term = sum_columns(outer(third, grad_gates))
    grad_third_pre, gain_three, shift_three = norm_back(third_pre, gains[2], grad_third)

    grad_ffn = with_partner(grad_third_pre.astype(BF))
    down_term = outer(hidden, grad_ffn)
    down_term = down_term.reshape(groups, down_rows, 2, part)
    down_term = jnp.moveaxis(down_term, 2, 1).reshape(groups, -1, part)
    down_term = lines.scatter(down_term)
    grad_hidden = dot_t(grad_ffn, down)
    grad_hidden_pre = jax.vjp(
        lambda value: jax.nn.gelu(value, approximate=False), hidden_pre
    )[1](grad_hidden)[0].astype(BF)

    def shard_blocks(terms):
        return jnp.concatenate([t.reshape(groups, rows_of, part) for t in terms], 1)

    up_term = outer(second_all, grad_hidden_pre)
    up_term = lines.scatter(
        shard_blocks([up_term[:, i * part : (i + 1) * part] for i in range(parts_up)] + [gate_term])
    )
    grad_second = grad_third_pre + sum_rows(dot_t(grad_hidden_pre, up))
    grad_second_pre, gain_two, shift_two = norm_back(second_pre, gains[1], grad_second)

    grad_low = grad_second_pre.astype(BF)
    self_out_term = sum_columns(outer(self_o, grad_low))
    grad_mixed = rows_to_heads(dot_t(grad_low, self_out).astype(BF))
    grads = attend_back(self_p, self_q, self_k, self_v, grad_mixed)
    self_term = lines.scatter(shard_blocks([outer(first_all, g) for g in grads] + [self_out_term]))
    grad_first = grad_second_pre + sum_rows(
        dot_t(grads[0], self_in[0]) + dot_t(grads[1], self_in[1]) + dot_t(grads[2], self_in[2])
    )
    grad_first_pre, gain_one, shift_one = norm_back(first_pre, gains[0], grad_first)

    grad_low = grad_first_pre.astype(BF)
    cross_out_term = sum_columns(outer(cross_o, grad_low))
    grad_mixed = rows_to_heads(dot_t(grad_low, cross_out).astype(BF))
    grads = attend_back(cross_p, cross_q, cross_k, cross_v, grad_mixed)
    terms = jnp.stack(
        [gain_one, gain_two, gain_three, shift_one, shift_two, shift_three, bias_term]
    )
    terms = (terms + swap_core(terms)).astype(BF)
    terms = jnp.moveaxis(terms.reshape(7, groups, rows_of), 1, 0).reshape(groups, -1)
    terms = jnp.pad(terms, ((0, 0), (0, small_rows * part - 7 * rows_of)))
    cross_term = lines.scatter(
        jnp.concatenate(
            [
                shard_blocks(
                    [
                        outer(asked, grads[0]),
                        outer(shown, grads[1]),
                        outer(shown, grads[2]),
                        cross_out_term,
                    ]
                ),
                terms.reshape(groups, small_rows, part),
            ],
            1,
        )
    )
    grad_asked = dot_t(grads[0], cross_in[0])
    grad_shown = dot_t(grads[1], cross_in[1]) + dot_t(grads[2], cross_in[2])
    grad_asked = grad_first_pre + sum_rows(grad_asked)
    grad_shown = sum_rows(grad_shown)
    sent = swap_kind(jnp.concatenate([grad_asked[1:], grad_shown[1:]], 0).astype(BF)).astype(F32)
    streams_grad = in_order(
        kind, (grad_asked[:1] + sent[1:])[None], (grad_shown[:1] + sent[:1])[None], 0
    )

    def everywhere(value):
        kinds = in_order(kind, value[None], swap_kind(value)[None], 0)
        return in_order(half, kinds[:, None], swap_core(kinds)[:, None], 1)

    def wide(value, lead):
        value = value.reshape((2, 2, lead, -1, part))
        return jnp.moveaxis(value, 1, 3).reshape(2, lead, -1, width).astype(F32)

    cross_term = everywhere(cross_term)
    self_term = everywhere(self_term)
    up_term = everywhere(up_term)
    down_term = everywhere(down_term)
    three, four = 3 * rows_of, 4 * rows_of
    attn_in_grad = jnp.stack(
        [wide(cross_term[:, :, :three], 3), wide(self_term[:, :, :three], 3)], 1
    )
    attn_out_grad = jnp.stack(
        [wide(cross_term[:, :, three:four], 1)[:, 0], wide(self_term[:, :, three:], 1)[:, 0]], 1
    )
    gate_grad = wide(up_term[:, :, parts_up * rows_of :], 1)[:, 0]
    up_grad = up_term[:, :, : parts_up * rows_of].reshape(2, 2, parts_up, rows_of, part)
    up_grad = jnp.moveaxis(up_grad, 2, 3).reshape(2, 2, rows_of, groups, hid_half)
    up_grad = jnp.moveaxis(up_grad, 1, 3).reshape(ffn_up.shape).astype(F32)
    down_grad = down_term.reshape(2, 2, 2, down_rows, part)
    down_grad = jnp.moveaxis(down_grad, 2, 3).reshape(ffn_down.shape).astype(F32)
    tail = cross_term[:, 0, four:].reshape(2, -1)[:, : 7 * rows_of]
    tail = tail.reshape(2, 7, rows_of).astype(F32)
    return (
        mixed_streams,
        streams_grad,
        attn_in_grad,
        attn_out_grad,
        up_grad,
        down_grad,
        gate_grad,
        tail[0, 6] + tail[1, 6],
        tail[:, :3],
        tail[:, 3:6],
    )


def solution(mesh):
    lines = Lines(lines_of(mesh))
    rows = P(None, ("fsdp", "dp"), None, None)
    weights = (
        P(None, None, None, "fsdp", None),
        P(None, None, "fsdp", None),
        P(None, "fsdp", None),
        P(None, "fsdp", None),
        P(None, "fsdp", None),
        P("fsdp"),
        P(None, None, "fsdp"),
        P(None, None, "fsdp"),
    )
    return jax.shard_map(
        lambda *args: body(lines, *args),
        mesh=mesh,
        in_specs=(rows, P(None, ("fsdp", "dp"), None)) + weights + (rows,),
        out_specs=(rows, rows) + weights,
        check_vma=False,
    )
```
